32 devices in a mesh: chain: 4 (over y, core), dp: 8 (over z, x).
Axes of the slice: x: 2, y: 2, z: 4, core: 2. Of those that a mesh axis runs over, the one named last changes fastest.
Arguments:
- train_features: float32 [256, 8, 8, 64], P('dp'), may hold values from -20 to 20
- train_labels: int32 [256], P('dp'), may hold values from 0 to 9
- test_features: float32 [512, 8, 8, 64], P('dp'), may hold values from -6 to 6
- conv_first: float32 [4, 9, 64, 64], P('chain'), may hold values from -0.25 to 0.25
- conv_second: float32 [4, 9, 64, 64], P('chain'), may hold values from -0.25 to 0.25
- norm_params: float32 [4, 6, 64], P('chain'), may hold values from -3 to 3
- head_weight: float32 [4, 64, 10], P('chain'), may hold values from -0.75 to 0.75
- head_bias: float32 [4, 10], P('chain'), may hold values from -3 to 3
- mom_first: float32 [4, 9, 64, 64], P('chain'), may hold values from -6 to 6
- mom_second: float32 [4, 9, 64, 64], P('chain'), may hold values from -6 to 6
- mom_norm: float32 [4, 6, 64], P('chain'), may hold values from -6 to 6
- mom_head: float32 [4, 64, 10], P('chain'), may hold values from -6 to 6
- mom_bias: float32 [4, 10], P('chain'), may hold values from -6 to 6
- step_size: float32 [4], P('chain'), may hold values from 0.001 to 0.003
Outputs:
- predictive: float32 [512, 10], P('dp')
- hamiltonians: float32 [4, 2], P('chain')
- potentials: float32 [4, 2], P('chain')
- forces: float32 [4, 2, 9, 64, 64], P('chain', None, None, 'dp')
The draws below stay inside these ranges and needn't reach their ends.
All inputs are finite; a program needn't handle non-finite values.
Results may differ from the reference program's by a relative error of at most 0.0003.
Values sent between devices are 32-bit elements; how exact they have to be, the bound alone decides.
A program may use at most 128 MiB of HBM per device.

```python
import math
import jax
import jax.numpy as jnp
from jax import lax

CH = 64
CLASSES = 10
SIDE = 8
TAPS = 9
IMAGES = 256
TESTS = 512
CHAINS = 4


def draw_train_features(key, part):
    first_key = jax.random.fold_in(key, 11)
    place = jnp.arange(IMAGES, dtype=jnp.float32) / jnp.float32(max(IMAGES - 1, 1))
    scale = jnp.exp(place * math.log(4.0))
    values = jax.random.truncated_normal(first_key, -4.0, 4.0, (IMAGES, SIDE, SIDE, CH), jnp.float32)
    return values * scale[:, None, None, None]


def with_ends(drawn, stream_key, low, largest):
    longest = drawn.shape.index(max(drawn.shape))
    spots = []
    for shift in (0, 1):
        where = [jax.random.randint(jax.random.fold_in(stream_key, axis), (), 0, length) for axis, length in enumerate(drawn.shape)]
        where[longest] = (where[longest] + shift) % drawn.shape[longest]
        spots.append(tuple(where))
    return drawn.at[spots[0]].set(low).at[spots[1]].set(largest)


def shard_levels(key, dims, cuts, smallest, largest):
    def one(dim, parts):
        steps = jax.random.uniform(jax.random.fold_in(jax.random.fold_in(key, 6), dim), (parts,), jnp.float32, smallest / len(cuts), largest / len(cuts))
        return jnp.repeat(jnp.exp(steps), dims[dim] // parts).reshape((-1,) + (1,) * (len(dims) - dim - 1))

    factor_of = one(*cuts[0])
    for cut in cuts[1:]:
        factor_of = factor_of * one(*cut)
    return factor_of


def noise(own_key, extent, deviation, reach, cuts=(), kind=jnp.bfloat16):
    loudness = shard_levels(own_key, extent, cuts, -0.22, 0.18) if cuts else 1.0
    entries = jax.random.normal(own_key, extent, jnp.float32) * deviation * loudness
    return jnp.minimum(jnp.maximum(entries, -reach), reach).astype(kind)


def setup_inputs(seed: int = 0) -> dict:
    arg_keys = jax.random.split(jax.random.key(seed), 15)
    train_features = draw_train_features(jax.random.fold_in(arg_keys[14], 71), 0)
    train_labels = with_ends(jax.random.randint(arg_keys[1], (IMAGES,), 0, CLASSES), jax.random.fold_in(arg_keys[1], 1), 0, CLASSES - 1).astype(jnp.int32)
    test_features = noise(arg_keys[2], (TESTS, SIDE, SIDE, CH), 1.0, 6.0, ((0, 8),), jnp.float32)
    conv_first = noise(arg_keys[3], (CHAINS, TAPS, CH, CH), (TAPS * CH) ** -0.5, 0.25, ((0, 4),), jnp.float32)
    conv_second = noise(arg_keys[4], (CHAINS, TAPS, CH, CH), (TAPS * CH) ** -0.5, 0.25, ((0, 4),), jnp.float32)
    norm_params = noise(arg_keys[5], (CHAINS, 6, CH), 0.5, 3.0, ((0, 4),), jnp.float32)
    head_weight = noise(arg_keys[6], (CHAINS, CH, CLASSES), CH ** -0.5, 0.75, ((0, 4),), jnp.float32)
    head_bias = noise(arg_keys[7], (CHAINS, CLASSES), 0.5, 3.0, ((0, 4),), jnp.float32)
    mom_first = noise(arg_keys[8], (CHAINS, TAPS, CH, CH), 1.0, 6.0, ((0, 4),), jnp.float32)
    mom_second = noise(arg_keys[9], (CHAINS, TAPS, CH, CH), 1.0, 6.0, ((0, 4),), jnp.float32)
    mom_norm = noise(arg_keys[10], (CHAINS, 6, CH), 1.0, 6.0, ((0, 4),), jnp.float32)
    mom_head = noise(arg_keys[11], (CHAINS, CH, CLASSES), 1.0, 6.0, ((0, 4),), jnp.float32)
    mom_bias = noise(arg_keys[12], (CHAINS, CLASSES), 1.0, 6.0, ((0, 4),), jnp.float32)
    step_size = jnp.clip(jnp.exp(math.log(0.003) - 1.09861225 * jax.random.uniform(arg_keys[13], (CHAINS,), jnp.float32) ** shard_levels(arg_keys[13], (CHAINS,), ((0, 4),), -0.2, 0.2)), 0.001, 0.003)
    return {"train_features": train_features, "train_labels": train_labels, "test_features": test_features, "conv_first": conv_first, "conv_second": conv_second, "norm_params": norm_params, "head_weight": head_weight, "head_bias": head_bias, "mom_first": mom_first, "mom_second": mom_second, "mom_norm": mom_norm, "mom_head": mom_head, "mom_bias": mom_bias, "step_size": step_size}


highest = lax.Precision.HIGHEST
epsilon = 1e-06

def conv_layer(inputs, kernel):
    height = inputs.shape[1]
    breadth = inputs.shape[2]
    padded = jnp.pad(inputs, ((0, 0), (1, 1), (1, 1), (0, 0)))
    total = jnp.zeros(inputs.shape[:3] + (kernel.shape[2],), jnp.float32)
    for offset in range(9):
        row_off = offset // 3
        col_off = offset % 3
        window = padded[:, row_off:row_off + height, col_off:col_off + breadth, :]
        total = total + jnp.einsum('bhwc,cd->bhwd', window, kernel[offset], precision=highest)
    return total

def normalize(values, gain, shift):
    moment = lax.optimization_barrier(jnp.mean(values * values, axis=(1, 2), keepdims=True))
    return values * lax.rsqrt(moment + epsilon) * gain + shift

def network(params, features):
    kernel_one, kernel_two, norms, weights, biases = params
    hidden = jnp.maximum(normalize(conv_layer(features, kernel_one), norms[0], norms[1]), norms[2])
    branch = normalize(conv_layer(hidden, kernel_two), norms[3], norms[4])
    joined = jnp.maximum(features + branch, norms[5])
    pooled = lax.optimization_barrier(jnp.mean(joined, axis=(1, 2)))
    return jnp.dot(pooled, weights, precision=highest) + biases

def cross_sum(params, features, labels):
    logits = network(params, features)
    onehot = (labels[:, None] == jnp.arange(logits.shape[1], dtype=jnp.int32)[None, :]).astype(jnp.float32)
    return jnp.sum(jax.nn.logsumexp(logits, axis=1) - lax.optimization_barrier(jnp.sum(onehot * logits, axis=1)))

def squares_half(params):
    total = jnp.float32(0.0)
    for tensor in params:
        total = total + 0.5 * jnp.sum(tensor * tensor)
    return total

def reference(train_features, train_labels, test_features, conv_first, conv_second, norm_params, head_weight, head_bias, mom_first, mom_second, mom_norm, mom_head, mom_bias, step_size):

    def potential(position):
        return cross_sum(position, train_features, train_labels) + squares_half(position)
    value_grad = jax.value_and_grad(potential)

    def one_chain(chain_args):
        position = tuple(chain_args[0:5])
        start_mom = tuple(chain_args[5:10])
        stride = chain_args[10]
        energy_start, grad_start = value_grad(position)
        momentum = tuple((mom_val - 0.5 * stride * grad_val for mom_val, grad_val in zip(start_mom, grad_start)))
        position = tuple((pos_val + stride * mom_val for pos_val, mom_val in zip(position, momentum)))
        unused, grad_middle = value_grad(position)
        momentum = tuple((mom_val - stride * grad_val for mom_val, grad_val in zip(momentum, grad_middle)))
        position = tuple((pos_val + stride * mom_val for pos_val, mom_val in zip(position, momentum)))
        energy_end, grad_end = value_grad(position)
        momentum = tuple((mom_val - 0.5 * stride * grad_val for mom_val, grad_val in zip(momentum, grad_end)))
        pair = jnp.stack([energy_start + squares_half(start_mom), energy_end + squares_half(momentum)])
        pot_pair = jnp.stack([energy_start, energy_end])
        force_one = 0.5 * grad_start[0] + grad_middle[0] + 0.5 * grad_end[0]
        force_two = 0.5 * grad_start[1] + grad_middle[1] + 0.5 * grad_end[1]
        probs = jax.nn.softmax(network(position, test_features), axis=-1)
        return (probs, pair, pot_pair, jnp.stack([force_one, force_two]))
    probs_all, pairs, pot_pairs, force_all = lax.map(one_chain, (conv_first, conv_second, norm_params, head_weight, head_bias, mom_first, mom_second, mom_norm, mom_head, mom_bias, step_size))
    predictive = lax.optimization_barrier(jnp.sum(probs_all, axis=0)) / CHAINS
    return (predictive, pairs, pot_pairs, force_all)
```

```python
import functools

import jax
import jax.numpy as jnp
from jax import lax
from jax.experimental import pallas as pl
from jax.experimental.pallas import tpu as pltpu
from jax.sharding import PartitionSpec as P

MESH = pl.DeviceIdType.MESH
HIGHEST = lax.Precision.HIGHEST
EPS = 1e-6
CH = 64
TAPS = 9
SMALL = 16
F32 = jnp.float32
BF16 = jnp.bfloat16


def split(value):
    high = value.astype(BF16)
    return high, (value - high.astype(F32)).astype(BF16)


def mm(left, right):
    return jnp.dot(left, right, preferred_element_type=F32)


def put_weights(ref, taps):
    zero = jnp.zeros((CH, CH), F32)
    for a in range(3):
        mine = taps[3 * a : 3 * a + 3]
        left = jnp.concatenate(mine + [zero], axis=0)
        right = jnp.concatenate([zero] + mine, axis=0)
        high, low = split(jnp.concatenate([left, right], axis=1))
        ref[256 * a : 256 * a + 256, 0:128] = high
        ref[256 * a : 256 * a + 256, 128:256] = low


def clear(ref):
    ref[...] = jnp.zeros_like(ref)


def load_maps(raw, out, images):
    height, width = raw.shape[1], raw.shape[2]
    flat = raw.reshape(images * height * width, CH)
    for p in range(width // 2):
        for h in range(height):
            left, right = [flat[pl.ds(h * width + 2 * p + q, images, stride=height * width), :] for q in (0, 1)]
            out[p, h * images : (h + 1) * images, :] = jnp.concatenate([left, right], axis=1)


def put_windows(hs, ls, blocks, images):
    last = len(blocks) - 1
    for p, block in enumerate(blocks):
        rows = slice(images, images + block.shape[0])
        for ref, val in zip((hs, ls), split(pltpu.roll(block, CH, 1))):
            ref[p, rows, 64:128] = val[:, 64:128]
            ref[p, rows, 128:192] = val[:, 0:64]
            if p < last:
                ref[p + 1, rows, 0:64] = val[:, 0:64]
            if p > 0:
                ref[p - 1, rows, 192:256] = val[:, 64:128]


def put_turned(ref, blocks):
    for p, block in enumerate(blocks):
        rows = block.shape[0]
        high, low = split(block.T)
        ref[0:128, p * rows : (p + 1) * rows] = high
        ref[128:256, p * rows : (p + 1) * rows] = low


def conv(hs, ls, weights, images):
    rows = hs.shape[1] - 2 * images
    edge = jnp.zeros((images, 128), F32)
    highs = jnp.concatenate([weights[256 * a : 256 * a + 256, 0:128] for a in range(3)], axis=1)
    outs = []
    for p in range(hs.shape[0]):
        window = jnp.concatenate([hs[p, a * images : a * images + rows, :] for a in range(3)], axis=1)
        both = mm(window, weights[...])
        rest = mm(ls[p, images : images + rows, :], highs)
        down = jnp.concatenate([edge, rest[: rows - images, 0:128]], axis=0)
        up = jnp.concatenate([rest[images:, 256:384], edge], axis=0)
        outs.append(both[:, :128] + (both[:, 128:] + (rest[:, 128:256] + down + up)))
    return outs


def kernel_grad(turned, hs, ls, images):
    rows = hs.shape[1] - 2 * images
    grads = []
    for a in range(3):
        start = (2 - a) * images

        def window(ref):
            return jnp.concatenate([ref[p, start : start + rows, :] for p in range(ref.shape[0])], axis=0)

        both = mm(turned[...], window(hs))
        total = both[:128] + (both[128:] + mm(turned[0:128, :], window(ls)))
        for b in range(3):
            grads.append(total[0:64, (2 - b) * 64 : (3 - b) * 64] + total[64:128, (3 - b) * 64 : (4 - b) * 64])
    return grads


def image_sum(blocks, images):
    totals = []
    for block in blocks:
        total = block[0:images]
        for h in range(1, block.shape[0] // images):
            total = total + block[h * images : (h + 1) * images]
        totals.append(total)
    while len(totals) > 1:
        totals = [left + right for left, right in zip(totals[::2], totals[1::2])]
    return totals[0] + pltpu.roll(totals[0], CH, 1)


def spread(value, rows):
    return jnp.concatenate([value] * (rows // value.shape[0]), axis=0)


def wide(row):
    return jnp.concatenate([row, row], axis=1)


def masked(value, bound, full, half):
    return jnp.where(value > bound, full, jnp.where(value == bound, half, 0.0))


def over_images(value):
    return jnp.sum(value, axis=0, keepdims=True)[:, 0:64]


def load_taps(theta):
    shards = theta.shape[0]
    per = CH // shards

    def tap(t):
        lane = 64 * (t % 2)
        return jnp.concatenate(
            [theta[s, t // 2 * per : (t // 2 + 1) * per, lane : lane + 64] for s in range(shards)], axis=0
        )

    return [tap(t) for t in range(TAPS)]


def own_share(taps, me, per):
    rows = pl.ds(pl.multiple_of(me * per, per), per)
    blocks = [jnp.concatenate([taps[0, 2 * i, rows, :], taps[0, 2 * i + 1, rows, :]], axis=1) for i in range(4)]
    last = taps[0, 8, rows, :]
    return jnp.concatenate(blocks + [jnp.concatenate([last, jnp.zeros_like(last)], axis=1)], axis=0)


def put_grads(out, grads, extra):
    shards = out.shape[0]
    per = CH // shards
    for i in range(5):
        both = jnp.concatenate([grads[2 * i], grads[2 * i + 1] if i < 4 else jnp.zeros((CH, CH), F32)], axis=1)
        for s in range(shards):
            piece = both[s * per : (s + 1) * per]
            if i == 4 and extra is not None:
                tail = jnp.concatenate([extra, jnp.zeros((per - 1, CH), F32)], axis=0)
                piece = jnp.concatenate([piece[:, 0:64], tail], axis=1)
            out[s, i * per : (i + 1) * per, :] = piece


def put_forces(forces, which, force, per):
    for t in range(TAPS):
        lane = 64 * (t % 2)
        forces[0, which, t] = force[t // 2 * per : (t // 2 + 1) * per, lane : lane + 64]


def head_rows(small):
    return jnp.concatenate([small[3:8, 0:64], small[3:8, 64:128], jnp.zeros((6, 64), F32)], axis=0)


def small_block(norms, head):
    return jnp.concatenate(
        [jnp.concatenate([norms[0:3], norms[3:6]], axis=1), jnp.concatenate([head[0:5], head[5:10]], axis=1)], axis=0
    )


def bias_rows(bias):
    return jnp.concatenate([jnp.concatenate([bias, jnp.zeros((1, 112), F32)], axis=1), jnp.zeros((7, 128), F32)], axis=0)


def pack_small(norms, head, bias, row):
    classes = head.shape[0]
    zero = jnp.zeros((1, 64), F32)
    row[...] = jnp.zeros_like(row)
    row[0:1, 0:classes] = bias[...]
    lines = [head[k] for k in range(classes)] + [zero] * (16 - classes)
    block = small_block(jnp.concatenate([norms[k] for k in range(6)], axis=0), jnp.concatenate(lines, axis=0))
    return jnp.concatenate([block, bias_rows(row[0:1, 0:16])], axis=0)


def norm_rows(small):
    return [wide(small[k % 3 : k % 3 + 1, 64 * (k // 3) : 64 * (k // 3) + 64]) for k in range(6)]


def classify(pooled, small):
    head = head_rows(small)
    logits = lax.dot_general(
        pooled, head, (((1,), (1,)), ((), ())), precision=HIGHEST, preferred_element_type=F32
    ) + small[8:9, 0:16]
    return head, logits


def forward(x, small, images, hs, ls, ys, yl, w_one, put_two, keep=None):
    rows = x.shape[1]
    pixels = x.shape[0] * 2 * (rows // images)
    norms = norm_rows(small)
    c1 = conv(hs, ls, w_one, images)
    r1 = lax.rsqrt(image_sum([c * c for c in c1], images) / pixels + EPS)
    gain = spread(r1 * norms[0], rows)
    v1 = [c * gain + norms[1] for c in c1]
    y = [jnp.maximum(v, norms[2]) for v in v1]
    put_windows(ys, yl, y, images)
    if keep is not None:
        keep(y)
    c2 = conv(ys, yl, put_two(), images)
    r2 = lax.rsqrt(image_sum([c * c for c in c2], images) / pixels + EPS)
    gain = spread(r2 * norms[3], rows)
    t = [x[p] + (c * gain + norms[4]) for p, c in enumerate(c2)]
    pooled = (image_sum([jnp.maximum(v, norms[5]) for v in t], images) / pixels)[:, 0:64]
    return norms, c1, r1, v1, c2, r2, t, pooled


def soft(logits, classes):
    valid = lax.broadcasted_iota(jnp.int32, logits.shape, 1) < classes
    top = jnp.max(jnp.where(valid, logits, -jnp.inf), axis=1, keepdims=True)
    powers = jnp.where(valid, jnp.exp(jnp.where(valid, logits - top, 0.0)), 0.0)
    total = jnp.sum(powers, axis=1, keepdims=True)
    return powers / total, top + jnp.log(total)


def gradient(classes, x, hot, taps_one, taps_two, small, refs, send_small, send_first, send_second):
    xs, xl, ys, yl, gs, gl, w_one, w_two, w_back, turned_x, turned_y = refs
    rows = x.shape[1]
    images = hot.shape[0]
    pixels = x.shape[0] * 2 * (rows // images)
    put_weights(w_one, taps_one)

    def put_two():
        taps = taps_two()
        put_weights(w_two, taps)
        put_weights(w_back, [tap.T for tap in reversed(taps)])
        return w_two

    norms, c1, r1, v1, c2, r2, t, pooled = forward(
        x, small, images, xs, xl, ys, yl, w_one, put_two, lambda y: put_turned(turned_y, y)
    )
    head, logits = classify(pooled, small)
    probs, lse = soft(logits, classes)
    cross = jnp.sum(lse - jnp.sum(hot * logits, axis=1, keepdims=True), axis=0, keepdims=True)
    dlog = probs - hot
    dpool = jnp.dot(dlog, head, precision=HIGHEST, preferred_element_type=F32) / pixels
    dhead = lax.dot_general(dlog, pooled, (((0,), (0,)), ((), ())), precision=HIGHEST, preferred_element_type=F32)
    dbias = jnp.sum(dlog, axis=0, keepdims=True)
    full = wide(dpool)
    full, half = spread(full, rows), spread(0.5 * full, rows)
    dz = [masked(v, norms[5], full, half) for v in t]
    dz_sum = image_sum(dz, images)
    dz_u = r2 * image_sum([z * c for z, c in zip(dz, c2)], images)
    gain = spread(r2 * norms[3], rows)
    pull = spread(r2 * r2 * (dz_u * norms[3] / pixels), rows)
    put_windows(gs, gl, [z * gain - c * pull for z, c in zip(dz, c2)], images)
    dy = conv(gs, gl, w_back, images)
    dv = [masked(v, norms[2], d, 0.5 * d) for v, d in zip(v1, dy)]
    dv_sum = image_sum(dv, images)
    dv_u = r1 * image_sum([d * c for d, c in zip(dv, c1)], images)
    gain = spread(r1 * norms[0], rows)
    pull = spread(r1 * r1 * (dv_u * norms[0] / pixels), rows)
    put_windows(ys, yl, [d * gain - c * pull for d, c in zip(dv, c1)], images)
    dn1, dn4 = over_images(dv_sum), over_images(dz_sum)
    dn2 = over_images(image_sum(dy, images)) - dn1
    dn5 = pixels * over_images(dpool) - dn4
    send_small(small_block(jnp.concatenate([over_images(dv_u), dn1, dn2, over_images(dz_u), dn4, dn5], axis=0), dhead))
    send_first(
        kernel_grad(turned_x, ys, yl, images),
        jnp.concatenate([dbias, jnp.broadcast_to(cross, (1, 48))], axis=1),
    )
    send_second(kernel_grad(turned_y, gs, gl, images))


def greet(axes):
    barrier = pltpu.get_barrier_semaphore()
    count = 0
    for axis in axes:
        n = lax.axis_size(axis)
        me = lax.axis_index(axis)
        for k in range(1, n):
            pl.semaphore_signal(barrier, inc=1, device_id={axis: lax.rem(me + k, n)}, device_id_type=MESH)
        count += n - 1
    return lambda: pl.semaphore_wait(barrier, count)


def send_all(axis, source, slot, send_sem, recv_sem):
    n = lax.axis_size(axis)
    me = lax.axis_index(axis)
    copies = []
    for k in sorted(range(1, n), key=lambda k: -min(k, n - k)):
        peer = lax.rem(me + k, n)
        copy = pltpu.make_async_remote_copy(
            src_ref=source(peer), dst_ref=slot(me), send_sem=send_sem.at[k], recv_sem=recv_sem.at[k],
            device_id={axis: peer}, device_id_type=MESH,
        )
        copy.start()
        copies.append(copy)
    return copies


def finish(copies):
    for copy in copies:
        copy.wait_recv()
    for copy in copies:
        copy.wait_send()


def in_order(ref):
    total = ref[0]
    for s in range(1, ref.shape[0]):
        total = total + ref[s]
    return total


def all_sum(value):
    while value.ndim > 2:
        value = jnp.sum(value, axis=0)
    return jnp.sum(jnp.sum(value, axis=0, keepdims=True), axis=1, keepdims=True)


def square_sum(value):
    return all_sum(value * value)


def whole_kernel(classes, step, x_hbm, label_hbm, test_hbm, first_hbm, second_hbm, norms_hbm, head_hbm, bias_hbm,
                 mom_first_hbm, mom_second_hbm, mom_norm_hbm, mom_head_hbm, mom_bias_hbm,
                 mean, hamiltonians, potentials, forces,
                 x_raw, label_ref, test_raw, first, second, norms, head, bias,
                 mom_first, mom_second, mom_norm, mom_head, mom_bias, load_sem,
                 x_ref, test_ref, xs, xl, ys, yl, gs, gl, ts, tl, us, ul, w_one, w_two, w_back, turned_x, turned_y,
                 square, small_all, small_mom, out_small, out_first, out_second, got_small, got_first, got_second,
                 mine_first, mine_second, all_first, all_second, mom_a, mom_b, part, parts, probs_own, seen,
                 send_g, recv_g, send_t, recv_t, send_d, recv_d, send_e, recv_e):
    n = lax.axis_size("dp")
    me = lax.axis_index("dp")
    chain = lax.axis_index("chain")
    per = CH // n
    arrived = greet(("dp", "chain"))
    loads = [
        pltpu.make_async_copy(source, target, load_sem.at[i])
        for i, (source, target) in enumerate(
            (
                (x_hbm, x_raw), (first_hbm, first), (norms_hbm, norms), (head_hbm, head), (bias_hbm, bias),
                (label_hbm, label_ref), (second_hbm, second), (mom_first_hbm, mom_first), (mom_second_hbm, mom_second),
                (mom_norm_hbm, mom_norm), (mom_head_hbm, mom_head), (mom_bias_hbm, mom_bias), (test_hbm, test_raw),
            )
        )
    ]
    for load in loads:
        load.start()
    h = step[0]
    images = label_ref.shape[1]
    tests = mean.shape[0]
    for ref in (xs, xl, ys, yl, gs, gl, ts, tl, us, ul):
        clear(ref)
    for load in loads[0:6]:
        load.wait()
    load_maps(x_raw, x_ref, images)
    spots = jnp.broadcast_to(label_ref[...], (128, images)) == lax.broadcasted_iota(jnp.int32, (128, images), 0)
    hot = jnp.where(spots, 1.0, 0.0).T[:, 0:16]
    pairs = x_ref.shape[0]
    put_windows(xs, xl, [x_ref[p] for p in range(pairs)], images)
    small_all[0] = pack_small(norms, head, bias, square)
    for load in loads[6:]:
        load.wait()
    refs = (xs, xl, ys, yl, gs, gl, w_one, w_two, w_back, turned_x, turned_y)
    rows_of = lax.broadcasted_iota(jnp.int32, (5 * per, 128), 0)
    lanes_of = lax.broadcasted_iota(jnp.int32, (5 * per, 128), 1)
    real = jnp.logical_or(rows_of < 4 * per, lanes_of < 64)
    taps_one = [first[0, t] for t in range(TAPS)]
    taps_two = lambda: [second[0, t] for t in range(TAPS)]
    force_a = force_b = None
    share_a = share_b = None
    for stage, factor in enumerate((0.5, 1.0, 0.5)):
        small = small_all.at[stage]
        copies = {}

        def send(kind, out, got):
            copies[kind] = send_all("dp", out, lambda s: got.at[stage, s], send_g.at[stage, kind], recv_g.at[stage, kind])

        def send_small(block):
            if stage == 0:
                arrived()
            out_small[...] = block
            send(0, lambda s: out_small, got_small)

        def send_first(grads, extra):
            put_grads(out_first, grads, extra)
            send(1, lambda s: out_first.at[s], got_first)

        def send_second(grads):
            put_grads(out_second, grads, None)
            send(2, lambda s: out_second.at[s], got_second)

        if stage == 0:
            put_turned(turned_x, [x_ref[p] for p in range(pairs)])
        gradient(classes, x_ref, hot, taps_one, taps_two, small, refs, send_small, send_first, send_second)
        got_small[stage, me] = out_small[...]
        got_first[stage, me] = out_first[me]
        got_second[stage, me] = out_second[me]
        if stage == 0:
            small_mom[...] = pack_small(mom_norm, mom_head, mom_bias, square)
            share_a, share_b = own_share(first, me, per), own_share(second, me, per)
            mom_a[...], mom_b[...] = own_share(mom_first, me, per), own_share(mom_second, me, per)
            theta_squares = square_sum(first[0]) + square_sum(second[0]) + square_sum(small[...])
            mom_squares = square_sum(mom_first[0]) + square_sum(mom_second[0]) + square_sum(small_mom[...])
            load_maps(test_raw, test_ref, tests)
        if stage == 1:
            put_windows(ts, tl, [test_ref[p] for p in range(pairs)], tests)
        if stage == 2:
            pooled = forward(test_ref, small, tests, ts, tl, us, ul, w_one, lambda: w_two)[-1]
            probs = soft(classify(pooled, small)[1], classes)[0]
            probs_own[...] = jnp.concatenate([probs, jnp.zeros((tests, 112), F32)], axis=1)
            others = send_all("chain", lambda s: probs_own, lambda s: seen.at[s], send_d, recv_d)
            seen[chain] = probs_own[...]
            share_squares = jnp.sum(share_a * share_a, axis=0, keepdims=True) + jnp.sum(
                share_b * share_b, axis=0, keepdims=True
            )
        weight = 0.5 if stage != 1 else 1.0
        finish(copies[0])
        finish(copies[1])
        sums = in_order(got_first.at[stage])
        extras = sums[4 * per : 4 * per + 1, 64:128]
        grad_a = jnp.where(real, sums, 0.0) + share_a
        next_a = mom_a[...] - (factor * h) * grad_a
        theta_copies = {}
        if stage < 2:
            share_a = share_a + h * next_a
            mine_first[...] = share_a
            theta_copies[0] = send_all("dp", lambda s: mine_first, lambda s: all_first.at[stage, s],
                                       send_t.at[stage, 0], recv_t.at[stage, 0])
            all_first[stage, me] = share_a
            mom_a[...] = next_a
        force_a = weight * grad_a if force_a is None else force_a + weight * grad_a
        small_sums = jnp.concatenate([in_order(got_small.at[stage]), bias_rows(extras[:, 0:16])], axis=0)
        small_next = small_mom[...] - (factor * h) * (small_sums + small[...])
        if stage < 2:
            small_all[stage + 1] = small[...] + h * small_next
            small_mom[...] = small_next
        if stage == 0:
            energy_start = extras[:, 32:33] + 0.5 * theta_squares
        finish(copies[2])
        grad_b = in_order(got_second.at[stage]) + share_b
        next_b = mom_b[...] - (factor * h) * grad_b
        if stage < 2:
            share_b = share_b + h * next_b
            mine_second[...] = share_b
            theta_copies[1] = send_all("dp", lambda s: mine_second, lambda s: all_second.at[stage, s],
                                       send_t.at[stage, 1], recv_t.at[stage, 1])
            all_second[stage, me] = share_b
            mom_b[...] = next_b
        force_b = weight * grad_b if force_b is None else force_b + weight * grad_b
        if stage < 2:
            finish(theta_copies[0])
            taps_one = load_taps(all_first.at[stage])

            def taps_two(waited=theta_copies[1], theta=all_second.at[stage]):
                finish(waited)
                return load_taps(theta)

    kinetic = jnp.sum(next_a * next_a, axis=0, keepdims=True) + jnp.sum(next_b * next_b, axis=0, keepdims=True)
    part[...] = jnp.concatenate([kinetic, share_squares, jnp.zeros((6, 128), F32)], axis=0)
    copies = send_all("dp", lambda s: part, lambda s: parts.at[s], send_e, recv_e)
    parts[me] = part[...]
    put_forces(forces, 0, force_a, per)
    put_forces(forces, 1, force_b, per)
    finish(others)
    mean[...] = in_order(seen) / lax.axis_size("chain")
    small_squares = square_sum(small_all[2])
    kinetic_small = square_sum(small_next)
    finish(copies)
    both = in_order(parts)
    energy_end = extras[:, 32:33] + 0.5 * (all_sum(both[1:2]) + small_squares)
    pot = jnp.concatenate([energy_start, energy_end], axis=1)
    potentials[...] = pot
    hamiltonians[...] = pot + 0.5 * jnp.concatenate([mom_squares, all_sum(both[0:1]) + kinetic_small], axis=1)


def deliver_kernel(mean, hamiltonians, potentials, forces, mean_out, hamiltonians_out, potentials_out, forces_out):
    mean_out[...] = mean[...].T[0 : mean_out.shape[0]]
    hamiltonians_out[...] = hamiltonians[...]
    potentials_out[...] = potentials[...]
    forces_out[...] = forces[...]


def vmem():
    return pl.BlockSpec(memory_space=pltpu.VMEM)


def shards(train_features, train_labels, test_features, *rest):
    n = lax.axis_size("dp")
    chains = lax.axis_size("chain")
    per = CH // n
    classes = rest[3].shape[2]
    images, height, width, _ = train_features.shape
    tests = test_features.shape[0]
    first, second, norms, head, bias, mom_first, mom_second, mom_norm, mom_head, mom_bias, step_size = rest

    def lead(array, order):
        return jnp.transpose(array, order)

    arrays = (train_features, jnp.reshape(train_labels, (1, images)), test_features,
              first, second, lead(norms, (1, 0, 2)), lead(head, (2, 0, 1)), bias,
              mom_first, mom_second, lead(mom_norm, (1, 0, 2)), lead(mom_head, (2, 0, 1)), mom_bias)
    pairs = width // 2

    def shape(*dims):
        return jax.ShapeDtypeStruct(dims, F32)

    def buffer(*dims):
        return pltpu.VMEM(dims, F32)

    def maps(count):
        return pltpu.VMEM((pairs, (height + 2) * count, 256), BF16)

    def pair(*dims):
        return [pltpu.SemaphoreType.DMA(dims)] * 2

    results = pl.pallas_call(
        functools.partial(whole_kernel, classes),
        out_shape=(shape(tests, 128), shape(1, 2), shape(1, 2), shape(1, 2, TAPS, per, 64)),
        in_specs=[pl.BlockSpec(memory_space=pltpu.SMEM)] + [pl.BlockSpec(memory_space=pl.ANY)] * len(arrays),
        out_specs=[vmem()] * 4,
        scratch_shapes=[pltpu.VMEM(array.shape, array.dtype) for array in arrays]
        + [pltpu.SemaphoreType.DMA((len(arrays),))]
        + [buffer(pairs, height * images, 128), buffer(pairs, height * tests, 128)]
        + [maps(images)] * 6 + [maps(tests)] * 4 + [pltpu.VMEM((768, 256), BF16)] * 3
        + [pltpu.VMEM((256, pairs * height * images), BF16)] * 2
        + [buffer(8, 128), buffer(3, 16, 128), buffer(16, 128), buffer(8, 128), buffer(n, 5 * per, 128),
           buffer(n, 5 * per, 128), buffer(3, n, 8, 128), buffer(3, n, 5 * per, 128), buffer(3, n, 5 * per, 128),
           buffer(5 * per, 128), buffer(5 * per, 128), buffer(2, n, 5 * per, 128), buffer(2, n, 5 * per, 128),
           buffer(5 * per, 128), buffer(5 * per, 128),
           buffer(8, 128), buffer(n, 8, 128), buffer(tests, 128), buffer(chains, tests, 128)]
        + pair(3, 3, n) + pair(2, 2, n) + pair(chains) + pair(n),
        compiler_params=pltpu.CompilerParams(
            collective_id=0, has_side_effects=True, vmem_limit_bytes=56 << 20
        ),
        name="leapfrog",
    )(step_size, *arrays)
    mean, hamiltonians, potentials, forces = pl.pallas_call(
        deliver_kernel,
        out_shape=(shape(classes, tests), shape(1, 2), shape(1, 2), shape(1, 2, TAPS, per, 64)),
        in_specs=[vmem()] * 4,
        out_specs=[vmem()] * 4,
        name="deliver",
    )(*results)
    return mean.T, hamiltonians, potentials, forces


def solution(mesh):
    placed = (
        P("dp", None, None, None),
        P("dp"),
        P("dp", None, None, None),
        P("chain", None, None, None),
        P("chain", None, None, None),
        P("chain", None, None),
        P("chain", None, None),
        P("chain", None),
        P("chain", None, None, None),
        P("chain", None, None, None),
        P("chain", None, None),
        P("chain", None, None),
        P("chain", None),
        P("chain"),
    )
    return jax.shard_map(
        shards,
        mesh=mesh,
        in_specs=placed,
        out_specs=(
            P("dp", None),
            P("chain", None),
            P("chain", None),
            P("chain", None, None, "dp", None),
        ),
        check_vma=False,
    )
```

```python
import functools

import jax
import jax.numpy as jnp
from jax import lax
from jax.experimental import pallas as pl
from jax.experimental.pallas import tpu as pltpu
from jax.sharding import PartitionSpec as P

MESH = pl.DeviceIdType.MESH
HIGHEST = lax.Precision.HIGHEST
EPS = 1e-6
CH = 64
TAPS = 9
PARTS = 2
GROUPS = ((0, 0, 2), (0, 2, 5), (1, 0, 5))
SUMS = 9
F32 = jnp.float32
BF16 = jnp.bfloat16


def split(value):
    high = value.astype(BF16)
    return high, (value - high.astype(F32)).astype(BF16)


def mm(left, right):
    return jnp.dot(left, right, preferred_element_type=F32)


def put_weights(ref, taps):
    zero = jnp.zeros((CH, CH), F32)
    for a in range(3):
        mine = taps[3 * a : 3 * a + 3]
        left = jnp.concatenate([mine[1], mine[2], zero, mine[0]], axis=0)
        right = jnp.concatenate(mine + [zero], axis=0)
        high, low = split(jnp.concatenate([left, right], axis=1))
        ref[256 * a : 256 * a + 256, 0:128] = high
        ref[256 * a : 256 * a + 256, 128:256] = low


def clear_edges(ref, images):
    pairs, rows, _ = ref.shape
    block = jnp.zeros((images, 256), BF16)
    for p in range(pairs):
        ref[p, 0:images, :] = block
        ref[p, rows - images : rows, :] = block
    ref[0, :, 192:256] = jnp.zeros((rows, 64), BF16)
    ref[pairs - 1, :, 128:192] = jnp.zeros((rows, 64), BF16)


def load_maps(raw, outs, images):
    height, width = raw.shape[1], raw.shape[2]
    flat = raw.reshape(raw.shape[0] * height * width, CH)
    for part, out in enumerate(outs):
        base = part * images * height * width
        for p in range(width // 2):
            for h in range(height):
                start = base + h * width + 2 * p
                left, right = [flat[pl.ds(start + q, images, stride=height * width), :] for q in (0, 1)]
                out[p, h * images : (h + 1) * images, :] = jnp.concatenate([left, right], axis=1)


def put_windows(hs, ls, blocks, images):
    last = len(blocks) - 1
    halves = [split(block) for block in blocks]
    for p, both in enumerate(halves):
        rows = slice(images, images + both[0].shape[0])
        for ref, val in zip((hs, ls), both):
            ref[p, rows, 0:128] = val
            if p > 0:
                ref[p - 1, rows, 128:192] = val[:, 0:64]
            if p < last:
                ref[p + 1, rows, 192:256] = val[:, 64:128]
    return halves


def put_turned(ref, halves, part):
    for p, (high, low) in enumerate(halves):
        rows = high.shape[0]
        start = (part * len(halves) + p) * rows
        ref[0:128, start : start + rows] = high.T
        ref[128:256, start : start + rows] = low.T


def stacked(ref, start, rows):
    return jnp.concatenate([ref[p, start : start + rows, :] for p in range(ref.shape[0])], axis=0)


def conv(hs, ls, weights, images):
    pairs = hs.shape[0]
    rows = hs.shape[1] - 2 * images
    edge = jnp.zeros((images, 128), F32)
    highs = jnp.concatenate([weights[256 * a : 256 * a + 256, 0:128] for a in range(3)], axis=1)
    window = jnp.concatenate([stacked(hs, a * images, rows) for a in range(3)], axis=1)
    both_all = mm(window, weights[...])
    rest_all = mm(stacked(ls, images, rows), highs)
    outs = []
    for p in range(pairs):
        both = both_all[p * rows : (p + 1) * rows]
        rest = rest_all[p * rows : (p + 1) * rows]
        down = jnp.concatenate([edge, rest[: rows - images, 0:128]], axis=0)
        up = jnp.concatenate([rest[images:, 256:384], edge], axis=0)
        outs.append(both[:, :128] + (both[:, 128:] + (rest[:, 128:256] + down + up)))
    return outs


def kernel_grad(turned, his, los, images, taps_rows=range(3)):
    rows = his[0].shape[1] - 2 * images
    grads = []
    for a in taps_rows:
        start = (2 - a) * images
        both = mm(turned[...], jnp.concatenate([stacked(ref, start, rows) for ref in his], axis=0))
        rest = mm(turned[0:128, :], jnp.concatenate([stacked(ref, start, rows) for ref in los], axis=0))
        total = both[:128] + (both[128:] + rest)
        for b in range(3):
            left, right = (1, 0, 3)[b] * 64, (2 - b) * 64
            grads.append(total[0:64, left : left + 64] + total[64:128, right : right + 64])
    return grads


def image_sum(blocks, images):
    totals = []
    for block in blocks:
        total = block[0:images]
        for h in range(1, block.shape[0] // images):
            total = total + block[h * images : (h + 1) * images]
        totals.append(total)
    while len(totals) > 1:
        totals = [left + right for left, right in zip(totals[::2], totals[1::2])]
    return totals[0] + pltpu.roll(totals[0], CH, 1)


def spread(value, rows):
    return jnp.concatenate([value] * (rows // value.shape[0]), axis=0)


def wide(row):
    return jnp.concatenate([row, row], axis=1)


def masked(value, bound, full, half):
    return jnp.where(value > bound, full, jnp.where(value == bound, half, 0.0))


def over_images(value):
    return jnp.sum(value, axis=0, keepdims=True)[:, 0:64]


def block_rows(low, high, per):
    return min(high, 4) * per + (per // 2 if high == 5 else 0) - low * per


def folded(tap, per):
    return jnp.concatenate([tap[0 : per // 2], tap[per // 2 : per]], axis=1)


def load_taps(pieces):
    def tap(t):
        for low, high, theta in pieces:
            if low <= t // 2 < high:
                shards = theta.shape[0]
                per = CH // shards
                row = (t // 2 - low) * per
                if t == 8:
                    parts = [theta[s, row : row + per // 2, 64 * k : 64 * k + 64] for s in range(shards) for k in (0, 1)]
                else:
                    lane = 64 * (t % 2)
                    parts = [theta[s, row : row + per, lane : lane + 64] for s in range(shards)]
                return jnp.concatenate(parts, axis=0)

    return [tap(t) for t in range(TAPS)]


def own_share(taps, me, per, low, high):
    rows = pl.ds(pl.multiple_of(me * per, per), per)

    def block(i):
        if i == 4:
            return folded(taps[0, 8, rows, :], per)
        return jnp.concatenate([taps[0, 2 * i, rows, :], taps[0, 2 * i + 1, rows, :]], axis=1)

    return jnp.concatenate([block(i) for i in range(low, high)], axis=0)


def put_grads(out, grads, low, high):
    shards = out.shape[0]
    per = CH // shards
    for i in range(low, high):
        for s in range(shards):
            rows = slice(s * per, (s + 1) * per)
            if i == 4:
                piece = folded(grads[8][rows], per)
            else:
                piece = jnp.concatenate([grads[2 * i][rows], grads[2 * i + 1][rows]], axis=1)
            out[s, (i - low) * per : (i - low) * per + piece.shape[0], :] = piece


def put_forces(forces, force, per, which, low, high):
    for t in range(2 * low, min(2 * high, TAPS)):
        lane = 64 * (t % 2)
        row = (t // 2 - low) * per
        if t == 8:
            forces[0, which, t, 0 : per // 2] = force[row : row + per // 2, 0:64]
            forces[0, which, t, per // 2 : per] = force[row : row + per // 2, 64:128]
        else:
            forces[0, which, t] = force[row : row + per, lane : lane + 64]


def head_rows(small):
    return jnp.concatenate([small[3:8, 0:64], small[3:8, 64:128], jnp.zeros((6, 64), F32)], axis=0)


def small_block(norms, head):
    return jnp.concatenate(
        [jnp.concatenate([norms[0:3], norms[3:6]], axis=1), jnp.concatenate([head[0:5], head[5:10]], axis=1)], axis=0
    )


def bias_rows(bias):
    return jnp.concatenate([jnp.concatenate([bias, jnp.zeros((1, 112), F32)], axis=1), jnp.zeros((7, 128), F32)], axis=0)


def pack_small(norms, head, bias, row):
    classes = head.shape[0]
    zero = jnp.zeros((1, 64), F32)
    row[...] = jnp.zeros_like(row)
    row[0:1, 0:classes] = bias[...]
    lines = [head[k] for k in range(classes)] + [zero] * (16 - classes)
    block = small_block(jnp.concatenate([norms[k] for k in range(6)], axis=0), jnp.concatenate(lines, axis=0))
    return jnp.concatenate([block, bias_rows(row[0:1, 0:16])], axis=0)


def norm_rows(small):
    return [wide(small[k % 3 : k % 3 + 1, 64 * (k // 3) : 64 * (k // 3) + 64]) for k in range(6)]


def classify(pooled, small):
    head = head_rows(small)
    logits = lax.dot_general(
        pooled, head, (((1,), (1,)), ((), ())), precision=HIGHEST, preferred_element_type=F32
    ) + small[8:9, 0:16]
    return head, logits


def soft(logits, classes):
    valid = lax.broadcasted_iota(jnp.int32, logits.shape, 1) < classes
    top = jnp.max(jnp.where(valid, logits, -jnp.inf), axis=1, keepdims=True)
    powers = jnp.where(valid, jnp.exp(jnp.where(valid, logits - top, 0.0)), 0.0)
    total = jnp.sum(powers, axis=1, keepdims=True)
    return powers / total, top + jnp.log(total)


def first_half(x, norms, images, hs, ls, ys, yl, weights, out):
    rows = x.shape[1]
    pixels = x.shape[0] * 2 * (rows // images)
    c1 = out["c1"] = conv(hs, ls, weights, images)
    yield
    r1 = out["r1"] = lax.rsqrt(image_sum([c * c for c in c1], images) / pixels + EPS)
    gain = spread(r1 * norms[0], rows)
    v1 = out["v1"] = [c * gain + norms[1] for c in c1]
    y = [jnp.maximum(v, norms[2]) for v in v1]
    out["halves"] = put_windows(ys, yl, y, images)


def second_half(x, norms, images, ys, yl, weights, out):
    rows = x.shape[1]
    pixels = x.shape[0] * 2 * (rows // images)
    c2 = out["c2"] = conv(ys, yl, weights, images)
    yield
    r2 = out["r2"] = lax.rsqrt(image_sum([c * c for c in c2], images) / pixels + EPS)
    gain = out["gain2"] = spread(r2 * norms[3], rows)
    t = out["t"] = [x[p] + (c * gain + norms[4]) for p, c in enumerate(c2)]
    out["pooled"] = (image_sum([jnp.maximum(v, norms[5]) for v in t], images) / pixels)[:, 0:64]


def step(*phases):
    for phase in phases:
        next(phase, None)


def test_logits(x, small, images, refs):
    hs, ls, ys, yl, w_one, w_two = refs
    norms = norm_rows(small)
    outs = [{} for _ in x]
    ahead = [first_half(x[i], norms, images, hs[i], ls[i], ys[i], yl[i], w_one, outs[i]) for i in range(len(x))]
    after = [second_half(x[i], norms, images, ys[i], yl[i], w_two, outs[i]) for i in range(len(x))]
    step(*ahead)
    for i in range(len(x)):
        step(ahead[i], after[i])
    step(*after)
    return classify(jnp.concatenate([out["pooled"] for out in outs], axis=0), small)[1]


def part_gradient(classes, part, x, hot, small, norms, refs, out):
    xs, xl, ys, yl, gs, gl, w_one, w_two, w_back, turned_y = refs
    rows = x.shape[1]
    images = hot.shape[0]
    pixels = x.shape[0] * 2 * (rows // images)
    ahead = first_half(x, norms, images, xs, xl, ys, yl, w_one, out)
    step(ahead)
    yield
    step(ahead)
    put_turned(turned_y, out["halves"], part)
    yield
    after = second_half(x, norms, images, ys, yl, w_two, out)
    step(after)
    yield
    step(after)
    c1, r1, v1, c2, r2, t, pooled = [out[key] for key in ("c1", "r1", "v1", "c2", "r2", "t", "pooled")]
    head, logits = classify(pooled, small)
    probs, lse = soft(logits, classes)
    dlog = probs - hot
    dpool = jnp.dot(dlog, head, precision=HIGHEST, preferred_element_type=F32) / pixels
    full = wide(dpool)
    full, half = spread(full, rows), spread(0.5 * full, rows)
    dz = [masked(v, norms[5], full, half) for v in t]
    dz_sum = image_sum(dz, images)
    dz_u = r2 * image_sum([z * c for z, c in zip(dz, c2)], images)
    gain = out["gain2"]
    pull = spread(r2 * r2 * (dz_u * norms[3] / pixels), rows)
    put_windows(gs, gl, [z * gain - c * pull for z, c in zip(dz, c2)], images)
    yield
    dy = conv(gs, gl, w_back, images)
    yield
    dv = [masked(v, norms[2], d, 0.5 * d) for v, d in zip(v1, dy)]
    dv_sum = image_sum(dv, images)
    dv_u = r1 * image_sum([d * c for d, c in zip(dv, c1)], images)
    gain = spread(r1 * norms[0], rows)
    pull = spread(r1 * r1 * (dv_u * norms[0] / pixels), rows)
    put_windows(ys, yl, [d * gain - c * pull for d, c in zip(dv, c1)], images)
    dn1, dn4 = over_images(dv_sum), over_images(dz_sum)
    dn2 = over_images(image_sum(dy, images)) - dn1
    dn5 = pixels * over_images(dpool) - dn4
    out["norms"] = jnp.concatenate([over_images(dv_u), dn1, dn2, over_images(dz_u), dn4, dn5], axis=0)
    out["head"] = lax.dot_general(dlog, pooled, (((0,), (0,)), ((), ())), precision=HIGHEST, preferred_element_type=F32)
    out["bias"] = jnp.sum(dlog, axis=0, keepdims=True)
    out["cross"] = jnp.sum(lse - jnp.sum(hot * logits, axis=1, keepdims=True), axis=0, keepdims=True)


def gradient(classes, x, hots, taps_one, taps_two, small, refs, send_small, send_first, send_second):
    xs, xl, ys, yl, gs, gl, w_one, w_two, w_back, turned_x, turned_y = refs
    images = hots[0].shape[0]
    norms = norm_rows(small)
    outs = [{} for _ in x]
    put_weights(w_one, taps_one)
    parts = [
        part_gradient(classes, i, x[i], hots[i], small, norms,
                      (xs[i], xl[i], ys[i], yl[i], gs[i], gl[i], w_one, w_two, w_back, turned_y), outs[i])
        for i in range(len(x))
    ]
    step(*parts)
    step(*parts)
    taps = taps_two()
    put_weights(w_two, taps)
    step(*parts)
    put_weights(w_back, [tap.T for tap in reversed(taps)])
    step(*parts)
    send_second(kernel_grad(turned_y, gs, gl, images))
    step(*parts)
    step(*parts)
    total = {key: sum(out[key] for out in outs[1:]) + outs[0][key] for key in ("norms", "head", "bias", "cross")}
    extras = jnp.concatenate([total["bias"], jnp.broadcast_to(total["cross"], (1, 112))], axis=1)
    grads_one = kernel_grad(turned_x, ys, yl, images, range(2))
    send_first(0, grads_one)
    send_first(1, grads_one + kernel_grad(turned_x, ys, yl, images, range(2, 3)))
    send_small(jnp.concatenate([small_block(total["norms"], total["head"]), extras], axis=0))


def greet(axes):
    barrier = pltpu.get_barrier_semaphore()
    count = 0
    for axis in axes:
        n = lax.axis_size(axis)
        me = lax.axis_index(axis)
        for k in range(1, n):
            pl.semaphore_signal(barrier, inc=1, device_id={axis: lax.rem(me + k, n)}, device_id_type=MESH)
        count += n - 1
    return lambda: pl.semaphore_wait(barrier, count)


def send_all(axis, source, slot, send_sem, recv_sem):
    n = lax.axis_size(axis)
    me = lax.axis_index(axis)
    copies = []
    for k in sorted(range(1, n), key=lambda k: -min(k, n - k)):
        peer = lax.rem(me + k, n)
        copy = pltpu.make_async_remote_copy(
            src_ref=source(peer), dst_ref=slot(me), send_sem=send_sem.at[k], recv_sem=recv_sem.at[k],
            device_id={axis: peer}, device_id_type=MESH,
        )
        copy.start()
        copies.append(copy)
    return copies


def leave(copies):
    for copy in copies:
        copy.wait_send()


def arrive(copies):
    for copy in copies:
        copy.wait_recv()


def finish(copies):
    arrive(copies)
    leave(copies)


def in_order(ref):
    total = ref[0]
    for s in range(1, ref.shape[0]):
        total = total + ref[s]
    return total


def all_sum(value):
    while value.ndim > 2:
        value = jnp.sum(value, axis=0)
    return jnp.sum(jnp.sum(value, axis=0, keepdims=True), axis=1, keepdims=True)


def square_sum(value):
    return all_sum(value * value)


def whole_kernel(classes, step_size, x_hbm, label_hbm, test_hbm, first_hbm, second_hbm, norms_hbm, head_hbm, bias_hbm,
                 mom_first_hbm, mom_second_hbm, mom_norm_hbm, mom_head_hbm, mom_bias_hbm,
                 mean, hamiltonians, potentials, forces,
                 x_raw, label_ref, test_raw, first, second, norms, head, bias,
                 mom_first, mom_second, mom_norm, mom_head, mom_bias, load_sem,
                 x_ref, test_ref, xs, xl, ys, yl, gs, gl, ts, tl, us, ul, w_one, w_two, w_back, turned_x, turned_y,
                 square, small_all, small_mom, out_small, got_small, outs, gots, mines, alls, moms,
                 part, parts, probs_own, seen,
                 send_s, recv_s, send_g, recv_g, send_t, recv_t, send_d, recv_d, send_e, recv_e):
    loads = [
        pltpu.make_async_copy(source, target, load_sem.at[i])
        for i, (source, target) in enumerate(
            (
                (x_hbm, x_raw), (first_hbm, first), (norms_hbm, norms), (head_hbm, head), (bias_hbm, bias),
                (label_hbm, label_ref), (second_hbm, second), (mom_first_hbm, mom_first), (mom_second_hbm, mom_second),
                (mom_norm_hbm, mom_norm), (mom_head_hbm, mom_head), (mom_bias_hbm, mom_bias), (test_hbm, test_raw),
            )
        )
    ]
    for load in loads:
        load.start()
    n = lax.axis_size("dp")
    me = lax.axis_index("dp")
    chain = lax.axis_index("chain")
    per = CH // n
    arrived = greet(("dp", "chain"))
    h = step_size[0]
    images = label_ref.shape[1]
    some = images // PARTS
    tests = mean.shape[0]
    pairs = x_ref[0].shape[0]
    for ref in xs + xl + ys + yl + gs + gl:
        clear_edges(ref, some)
    for load in loads[0:6]:
        load.wait()
    load_maps(x_raw, x_ref, some)
    spots = jnp.broadcast_to(label_ref[...], (128, images)) == lax.broadcasted_iota(jnp.int32, (128, images), 0)
    hot = jnp.where(spots, 1.0, 0.0).T[:, 0:16]
    hots = [hot[i * some : (i + 1) * some] for i in range(PARTS)]
    for i in range(PARTS):
        put_turned(turned_x, put_windows(xs[i], xl[i], [x_ref[i][p] for p in range(pairs)], some), i)
    small_all[0] = pack_small(norms, head, bias, square)
    for load in loads[6:]:
        load.wait()
    refs = (xs, xl, ys, yl, gs, gl, w_one, w_two, w_back, turned_x, turned_y)
    kernels, kernel_moms = (first, second), (mom_first, mom_second)
    taps_one = [first[0, t] for t in range(TAPS)]
    taps_two = lambda: [second[0, t] for t in range(TAPS)]
    shares = [None] * len(GROUPS)
    force = [None] * len(GROUPS)
    kinetic = [None] * len(GROUPS)
    for stage, factor in enumerate((0.5, 1.0, 0.5)):
        small = small_all.at[stage]
        copies = {}

        def send_group(g, grads):
            put_grads(outs[g], grads, *GROUPS[g][1:])
            copies[g] = send_all("dp", lambda s: outs[g].at[s], lambda s: gots[g].at[stage, s],
                                 send_g.at[stage, g], recv_g.at[stage, g])

        def send_small(block):
            out_small[...] = block
            copies["small"] = send_all("dp", lambda s: out_small, lambda s: got_small.at[stage, s],
                                       send_s.at[stage], recv_s.at[stage])

        def send_first(g, grads):
            send_group(g, grads)

        def send_second(grads):
            if stage == 0:
                arrived()
            send_group(2, grads)

        gradient(classes, x_ref, hots, taps_one, taps_two, small, refs, send_small, send_first, send_second)
        got_small[stage, me] = out_small[...]
        for g in range(len(GROUPS)):
            gots[g][stage, me] = outs[g][me]
        if stage == 0:
            small_mom[...] = pack_small(mom_norm, mom_head, mom_bias, square)
            for g, (which, low, high) in enumerate(GROUPS):
                shares[g] = own_share(kernels[which], me, per, low, high)
                moms[g][...] = own_share(kernel_moms[which], me, per, low, high)
            theta_squares = square_sum(first[0]) + square_sum(second[0]) + square_sum(small[...])
            mom_squares = square_sum(mom_first[0]) + square_sum(mom_second[0]) + square_sum(small_mom[...])
            load_maps(test_raw, test_ref, tests // PARTS)
        if stage == 1:
            for ref in ts + tl + us + ul:
                clear_edges(ref, tests // PARTS)
            for i in range(PARTS):
                put_windows(ts[i], tl[i], [test_ref[i][p] for p in range(pairs)], tests // PARTS)
        if stage == 2:
            logits = test_logits(test_ref, small, tests // PARTS, (ts, tl, us, ul, w_one, w_two))
            probs = soft(logits, classes)[0]
            probs_own[...] = jnp.concatenate([probs, jnp.zeros((tests, 112), F32)], axis=1)
            others = send_all("chain", lambda s: probs_own, lambda s: seen.at[s], send_d, recv_d)
            seen[chain] = probs_own[...]
            share_squares = sum(jnp.sum(share * share, axis=0, keepdims=True) for share in shares)
        weight = 0.5 if stage != 1 else 1.0
        theta_copies = [None] * len(GROUPS)

        def take_group(g):
            which, low, high = GROUPS[g]
            finish(copies[g])
            sums = in_order(gots[g].at[stage])
            grad = sums + shares[g]
            following = moms[g][...] - (factor * h) * grad
            if stage < 2:
                shares[g] = shares[g] + h * following
                mines[g][...] = shares[g]
                theta_copies[g] = send_all("dp", lambda s: mines[g], lambda s: alls[g].at[stage, s],
                                           send_t.at[stage, g], recv_t.at[stage, g])
                alls[g][stage, me] = shares[g]
                moms[g][...] = following
            else:
                kinetic[g] = jnp.sum(following * following, axis=0, keepdims=True)
            force[g] = weight * grad if force[g] is None else force[g] + weight * grad

        for g in range(len(GROUPS)):
            take_group(g)
        finish(copies["small"])
        sums = in_order(got_small.at[stage])
        extras = sums[8:SUMS]
        small_sums = jnp.concatenate([sums[0:8], bias_rows(extras[:, 0:16])], axis=0)
        small_next = small_mom[...] - (factor * h) * (small_sums + small[...])
        if stage < 2:
            small_all[stage + 1] = small[...] + h * small_next
            small_mom[...] = small_next
        if stage == 0:
            energy_start = extras[:, 32:33] + 0.5 * theta_squares
        if stage < 2:
            def gathered(which, copies, stage):
                for g, group in enumerate(GROUPS):
                    if group[0] == which:
                        finish(copies[g])
                return load_taps([(low, high, alls[g].at[stage]) for g, (k, low, high) in enumerate(GROUPS) if k == which])

            taps_one = gathered(0, theta_copies, stage)
            taps_two = functools.partial(gathered, 1, theta_copies, stage)
    part[...] = jnp.concatenate([sum(kinetic), share_squares, jnp.zeros((6, 128), F32)], axis=0)
    copies = send_all("dp", lambda s: part, lambda s: parts.at[s], send_e, recv_e)
    parts[me] = part[...]
    for g, group in enumerate(GROUPS):
        put_forces(forces, force[g], per, *group)
    finish(others)
    mean[...] = in_order(seen) / lax.axis_size("chain")
    small_squares = square_sum(small_all[2])
    kinetic_small = square_sum(small_next)
    finish(copies)
    both = in_order(parts)
    energy_end = extras[:, 32:33] + 0.5 * (all_sum(both[1:2]) + small_squares)
    pot = jnp.concatenate([energy_start, energy_end], axis=1)
    potentials[...] = pot
    hamiltonians[...] = pot + 0.5 * jnp.concatenate([mom_squares, all_sum(both[0:1]) + kinetic_small], axis=1)


def deliver_kernel(mean, hamiltonians, potentials, forces, mean_out, hamiltonians_out, potentials_out, forces_out):
    mean_out[...] = mean[...].T[0 : mean_out.shape[0]]
    hamiltonians_out[...] = hamiltonians[...]
    potentials_out[...] = potentials[...]
    forces_out[...] = forces[...]


def vmem():
    return pl.BlockSpec(memory_space=pltpu.VMEM)


def shards(train_features, train_labels, test_features, *rest):
    n = lax.axis_size("dp")
    chains = lax.axis_size("chain")
    per = CH // n
    classes = rest[3].shape[2]
    images, height, width, _ = train_features.shape
    tests = test_features.shape[0]
    first, second, norms, head, bias, mom_first, mom_second, mom_norm, mom_head, mom_bias, step_size = rest

    def lead(array, order):
        return jnp.transpose(array, order)

    arrays = (train_features, jnp.reshape(train_labels, (1, images)), test_features,
              first, second, lead(norms, (1, 0, 2)), lead(head, (2, 0, 1)), bias,
              mom_first, mom_second, lead(mom_norm, (1, 0, 2)), lead(mom_head, (2, 0, 1)), mom_bias)
    pairs = width // 2

    def shape(*dims):
        return jax.ShapeDtypeStruct(dims, F32)

    def buffer(*dims):
        return pltpu.VMEM(dims, F32)

    def maps(count):
        return [pltpu.VMEM((pairs, (height + 2) * count // PARTS, 256), BF16)] * PARTS

    def pair(*dims):
        return [pltpu.SemaphoreType.DMA(dims)] * 2

    def groups(*lead_dims):
        return [buffer(*lead_dims, block_rows(low, high, per), 128) for _, low, high in GROUPS]

    results = pl.pallas_call(
        functools.partial(whole_kernel, classes),
        out_shape=(shape(tests, 128), shape(1, 2), shape(1, 2), shape(1, 2, TAPS, per, 64)),
        in_specs=[pl.BlockSpec(memory_space=pltpu.SMEM)] + [pl.BlockSpec(memory_space=pl.ANY)] * len(arrays),
        out_specs=[vmem()] * 4,
        scratch_shapes=[pltpu.VMEM(array.shape, array.dtype) for array in arrays]
        + [pltpu.SemaphoreType.DMA((len(arrays),))]
        + [[buffer(pairs, height * count // PARTS, 128)] * PARTS for count in (images, tests)]
        + [maps(images)] * 6 + [maps(tests)] * 4 + [pltpu.VMEM((768, 256), BF16)] * 3
        + [pltpu.VMEM((256, pairs * height * images), BF16)] * 2
        + [buffer(8, 128), buffer(3, 16, 128), buffer(16, 128), buffer(SUMS, 128), buffer(3, n, SUMS, 128),
           groups(n), groups(3, n), groups(), groups(2, n), groups(),
           buffer(8, 128), buffer(n, 8, 128), buffer(tests, 128), buffer(chains, tests, 128)]
        + pair(3, n) + pair(3, len(GROUPS), n) + pair(2, len(GROUPS), n) + pair(chains) + pair(n),
        compiler_params=pltpu.CompilerParams(
            collective_id=0, has_side_effects=True, vmem_limit_bytes=56 << 20
        ),
        name="leapfrog",
    )(step_size, *arrays)
    mean, hamiltonians, potentials, forces = pl.pallas_call(
        deliver_kernel,
        out_shape=(shape(classes, tests), shape(1, 2), shape(1, 2), shape(1, 2, TAPS, per, 64)),
        in_specs=[vmem()] * 4,
        out_specs=[vmem()] * 4,
        name="deliver",
    )(*results)
    return mean.T, hamiltonians, potentials, forces


def solution(mesh):
    placed = (
        P("dp", None, None, None),
        P("dp"),
        P("dp", None, None, None),
        P("chain", None, None, None),
        P("chain", None, None, None),
        P("chain", None, None),
        P("chain", None, None),
        P("chain", None),
        P("chain", None, None, None),
        P("chain", None, None, None),
        P("chain", None, None),
        P("chain", None, None),
        P("chain", None),
        P("chain"),
    )
    return jax.shard_map(
        shards,
        mesh=mesh,
        in_specs=placed,
        out_specs=(
            P("dp", None),
            P("chain", None),
            P("chain", None),
            P("chain", None, None, "dp", None),
        ),
        check_vma=False,
    )
```

```python
import functools

import jax
import jax.numpy as jnp
from jax import lax
from jax.experimental import pallas as pl
from jax.experimental.pallas import tpu as pltpu
from jax.sharding import PartitionSpec as P

MESH = pl.DeviceIdType.MESH
HIGHEST = lax.Precision.HIGHEST
EPS = 1e-6
CH = 64
TAPS = 9
PARTS = 2
GROUPS = ((0, 0, 2), (0, 2, 5), (1, 0, 5))
SUMS = 9
F32 = jnp.float32
BF16 = jnp.bfloat16


def split(value):
    high = value.astype(BF16)
    return high, (value - high.astype(F32)).astype(BF16)


def mm(left, right):
    return jnp.dot(left, right, preferred_element_type=F32)


def put_weights(ref, taps):
    zero = jnp.zeros((CH, CH), F32)
    for a in range(3):
        mine = taps[3 * a : 3 * a + 3]
        left = jnp.concatenate([mine[1], mine[2], zero, mine[0]], axis=0)
        right = jnp.concatenate(mine + [zero], axis=0)
        high, low = split(jnp.concatenate([left, right], axis=1))
        ref[256 * a : 256 * a + 256, 0:128] = high
        ref[256 * a : 256 * a + 256, 128:256] = low


def clear_edges(ref, images):
    pairs, rows, _ = ref.shape
    block = jnp.zeros((images, 256), BF16)
    for p in range(pairs):
        ref[p, 0:images, :] = block
        ref[p, rows - images : rows, :] = block
    ref[0, :, 192:256] = jnp.zeros((rows, 64), BF16)
    ref[pairs - 1, :, 128:192] = jnp.zeros((rows, 64), BF16)


def load_maps(raw, outs, images):
    height, width = raw.shape[1], raw.shape[2]
    flat = raw.reshape(raw.shape[0] * height * width, CH)
    for part, out in enumerate(outs):
        base = part * images * height * width
        for p in range(width // 2):
            for h in range(height):
                start = base + h * width + 2 * p
                left, right = [flat[pl.ds(start + q, images, stride=height * width), :] for q in (0, 1)]
                out[p, h * images : (h + 1) * images, :] = jnp.concatenate([left, right], axis=1)


def put_windows(hs, ls, blocks, images):
    last = len(blocks) - 1
    halves = [split(block) for block in blocks]
    for p, both in enumerate(halves):
        rows = slice(images, images + both[0].shape[0])
        for ref, val in zip((hs, ls), both):
            ref[p, rows, 0:128] = val
            if p > 0:
                ref[p - 1, rows, 128:192] = val[:, 0:64]
            if p < last:
                ref[p + 1, rows, 192:256] = val[:, 64:128]
    return halves


def put_turned(ref, halves, part):
    for p, (high, low) in enumerate(halves):
        rows = high.shape[0]
        start = (part * len(halves) + p) * rows
        ref[0:128, start : start + rows] = high.T
        ref[128:256, start : start + rows] = low.T


def stacked(ref, start, rows):
    return jnp.concatenate([ref[p, start : start + rows, :] for p in range(ref.shape[0])], axis=0)


def conv(hs, ls, weights, images):
    pairs = hs.shape[0]
    rows = hs.shape[1] - 2 * images
    edge = jnp.zeros((images, 128), F32)
    highs = jnp.concatenate([weights[256 * a : 256 * a + 256, 0:128] for a in range(3)], axis=1)
    window = jnp.concatenate([stacked(hs, a * images, rows) for a in range(3)], axis=1)
    both_all = mm(window, weights[...])
    rest_all = mm(stacked(ls, images, rows), highs)
    outs = []
    for p in range(pairs):
        both = both_all[p * rows : (p + 1) * rows]
        rest = rest_all[p * rows : (p + 1) * rows]
        down = jnp.concatenate([edge, rest[: rows - images, 0:128]], axis=0)
        up = jnp.concatenate([rest[images:, 256:384], edge], axis=0)
        outs.append(both[:, :128] + (both[:, 128:] + (rest[:, 128:256] + down + up)))
    return outs


def kernel_grad(turned, his, los, images, taps_rows=range(3)):
    rows = his[0].shape[1] - 2 * images
    grads = []
    for a in taps_rows:
        start = (2 - a) * images
        both = mm(turned[...], jnp.concatenate([stacked(ref, start, rows) for ref in his], axis=0))
        rest = mm(turned[0:128, :], jnp.concatenate([stacked(ref, start, rows) for ref in los], axis=0))
        total = both[:128] + (both[128:] + rest)
        for b in range(3):
            left, right = (1, 0, 3)[b] * 64, (2 - b) * 64
            grads.append(total[0:64, left : left + 64] + total[64:128, right : right + 64])
    return grads


def image_sum(blocks, images):
    totals = []
    for block in blocks:
        total = block[0:images]
        for h in range(1, block.shape[0] // images):
            total = total + block[h * images : (h + 1) * images]
        totals.append(total)
    while len(totals) > 1:
        totals = [left + right for left, right in zip(totals[::2], totals[1::2])]
    return totals[0] + pltpu.roll(totals[0], CH, 1)


def spread(value, rows):
    return jnp.concatenate([value] * (rows // value.shape[0]), axis=0)


def wide(row):
    return jnp.concatenate([row, row], axis=1)


def masked(value, bound, full, half):
    return jnp.where(value > bound, full, jnp.where(value == bound, half, 0.0))


def over_images(value):
    return jnp.sum(value, axis=0, keepdims=True)[:, 0:64]


def block_rows(low, high, per):
    return min(high, 4) * per + (per // 2 if high == 5 else 0) - low * per


def folded(tap, per):
    return jnp.concatenate([tap[0 : per // 2], tap[per // 2 : per]], axis=1)


def load_taps(pieces):
    def tap(t):
        for low, high, theta in pieces:
            if low <= t // 2 < high:
                shards = theta.shape[0]
                per = CH // shards
                row = (t // 2 - low) * per
                if t == 8:
                    parts = [theta[s, row : row + per // 2, 64 * k : 64 * k + 64] for s in range(shards) for k in (0, 1)]
                else:
                    lane = 64 * (t % 2)
                    parts = [theta[s, row : row + per, lane : lane + 64] for s in range(shards)]
                return jnp.concatenate(parts, axis=0)

    return [tap(t) for t in range(TAPS)]


def own_share(taps, me, per, low, high):
    rows = pl.ds(pl.multiple_of(me * per, per), per)

    def block(i):
        if i == 4:
            return folded(taps[0, 8, rows, :], per)
        return jnp.concatenate([taps[0, 2 * i, rows, :], taps[0, 2 * i + 1, rows, :]], axis=1)

    return jnp.concatenate([block(i) for i in range(low, high)], axis=0)


def put_grads(out, grads, low, high):
    shards = out.shape[0]
    per = CH // shards
    for i in range(low, high):
        for s in range(shards):
            rows = slice(s * per, (s + 1) * per)
            if i == 4:
                piece = folded(grads[8][rows], per)
            else:
                piece = jnp.concatenate([grads[2 * i][rows], grads[2 * i + 1][rows]], axis=1)
            out[s, (i - low) * per : (i - low) * per + piece.shape[0], :] = piece


def put_forces(forces, force, per, which, low, high):
    for t in range(2 * low, min(2 * high, TAPS)):
        lane = 64 * (t % 2)
        row = (t // 2 - low) * per
        if t == 8:
            forces[0, which, t, 0 : per // 2] = force[row : row + per // 2, 0:64]
            forces[0, which, t, per // 2 : per] = force[row : row + per // 2, 64:128]
        else:
            forces[0, which, t] = force[row : row + per, lane : lane + 64]


def head_rows(small):
    return jnp.concatenate([small[3:8, 0:64], small[3:8, 64:128], jnp.zeros((6, 64), F32)], axis=0)


def small_block(norms, head):
    return jnp.concatenate(
        [jnp.concatenate([norms[0:3], norms[3:6]], axis=1), jnp.concatenate([head[0:5], head[5:10]], axis=1)], axis=0
    )


def bias_rows(bias):
    return jnp.concatenate([jnp.concatenate([bias, jnp.zeros((1, 112), F32)], axis=1), jnp.zeros((7, 128), F32)], axis=0)


def pack_small(norms, head, bias, row):
    classes = head.shape[0]
    zero = jnp.zeros((1, 64), F32)
    row[...] = jnp.zeros_like(row)
    row[0:1, 0:classes] = bias[...]
    lines = [head[k] for k in range(classes)] + [zero] * (16 - classes)
    block = small_block(jnp.concatenate([norms[k] for k in range(6)], axis=0), jnp.concatenate(lines, axis=0))
    return jnp.concatenate([block, bias_rows(row[0:1, 0:16])], axis=0)


def norm_rows(small):
    return [wide(small[k % 3 : k % 3 + 1, 64 * (k // 3) : 64 * (k // 3) + 64]) for k in range(6)]


def classify(pooled, small):
    head = head_rows(small)
    logits = lax.dot_general(
        pooled, head, (((1,), (1,)), ((), ())), precision=HIGHEST, preferred_element_type=F32
    ) + small[8:9, 0:16]
    return head, logits


def soft(logits, classes):
    valid = lax.broadcasted_iota(jnp.int32, logits.shape, 1) < classes
    top = jnp.max(jnp.where(valid, logits, -jnp.inf), axis=1, keepdims=True)
    powers = jnp.where(valid, jnp.exp(jnp.where(valid, logits - top, 0.0)), 0.0)
    total = jnp.sum(powers, axis=1, keepdims=True)
    return powers / total, top + jnp.log(total)


def first_half(x, norms, images, hs, ls, ys, yl, weights, out):
    rows = x.shape[1]
    pixels = x.shape[0] * 2 * (rows // images)
    c1 = out["c1"] = conv(hs, ls, weights, images)
    yield
    r1 = out["r1"] = lax.rsqrt(image_sum([c * c for c in c1], images) / pixels + EPS)
    gain = spread(r1 * norms[0], rows)
    v1 = out["v1"] = [c * gain + norms[1] for c in c1]
    y = [jnp.maximum(v, norms[2]) for v in v1]
    out["halves"] = put_windows(ys, yl, y, images)


def second_half(x, norms, images, ys, yl, weights, out):
    rows = x.shape[1]
    pixels = x.shape[0] * 2 * (rows // images)
    c2 = out["c2"] = conv(ys, yl, weights, images)
    yield
    r2 = out["r2"] = lax.rsqrt(image_sum([c * c for c in c2], images) / pixels + EPS)
    gain = out["gain2"] = spread(r2 * norms[3], rows)
    t = out["t"] = [x[p] + (c * gain + norms[4]) for p, c in enumerate(c2)]
    out["pooled"] = (image_sum([jnp.maximum(v, norms[5]) for v in t], images) / pixels)[:, 0:64]


def step(*phases):
    for phase in phases:
        next(phase, None)


def test_logits(x, small, images, refs):
    hs, ls, ys, yl, w_one, w_two = refs
    norms = norm_rows(small)
    outs = [{} for _ in x]
    ahead = [first_half(x[i], norms, images, hs[i], ls[i], ys[i], yl[i], w_one, outs[i]) for i in range(len(x))]
    after = [second_half(x[i], norms, images, ys[i], yl[i], w_two, outs[i]) for i in range(len(x))]
    step(*ahead)
    for i in range(len(x)):
        step(ahead[i], after[i])
    step(*after)
    return classify(jnp.concatenate([out["pooled"] for out in outs], axis=0), small)[1]


def part_gradient(classes, part, x, hot, small, norms, refs, out):
    xs, xl, ys, yl, gs, gl, w_one, w_two, w_back, turned_y = refs
    rows = x.shape[1]
    images = hot.shape[0]
    pixels = x.shape[0] * 2 * (rows // images)
    ahead = first_half(x, norms, images, xs, xl, ys, yl, w_one, out)
    step(ahead)
    yield
    step(ahead)
    put_turned(turned_y, out["halves"], part)
    yield
    after = second_half(x, norms, images, ys, yl, w_two, out)
    step(after)
    yield
    step(after)
    c1, r1, v1, c2, r2, t, pooled = [out[key] for key in ("c1", "r1", "v1", "c2", "r2", "t", "pooled")]
    head, logits = classify(pooled, small)
    probs, lse = soft(logits, classes)
    dlog = probs - hot
    dpool = jnp.dot(dlog, head, precision=HIGHEST, preferred_element_type=F32) / pixels
    full = wide(dpool)
    full, half = spread(full, rows), spread(0.5 * full, rows)
    dz = [masked(v, norms[5], full, half) for v in t]
    dz_sum = image_sum(dz, images)
    dz_u = r2 * image_sum([z * c for z, c in zip(dz, c2)], images)
    gain = out["gain2"]
    pull = spread(r2 * r2 * (dz_u * norms[3] / pixels), rows)
    put_windows(gs, gl, [z * gain - c * pull for z, c in zip(dz, c2)], images)
    yield
    dy = conv(gs, gl, w_back, images)
    yield
    dv = [masked(v, norms[2], d, 0.5 * d) for v, d in zip(v1, dy)]
    dv_sum = image_sum(dv, images)
    dv_u = r1 * image_sum([d * c for d, c in zip(dv, c1)], images)
    gain = spread(r1 * norms[0], rows)
    pull = spread(r1 * r1 * (dv_u * norms[0] / pixels), rows)
    put_windows(ys, yl, [d * gain - c * pull for d, c in zip(dv, c1)], images)
    dn1, dn4 = over_images(dv_sum), over_images(dz_sum)
    dn2 = over_images(image_sum(dy, images)) - dn1
    dn5 = pixels * over_images(dpool) - dn4
    out["norms"] = jnp.concatenate([over_images(dv_u), dn1, dn2, over_images(dz_u), dn4, dn5], axis=0)
    out["head"] = lax.dot_general(dlog, pooled, (((0,), (0,)), ((), ())), precision=HIGHEST, preferred_element_type=F32)
    out["bias"] = jnp.sum(dlog, axis=0, keepdims=True)
    out["cross"] = jnp.sum(lse - jnp.sum(hot * logits, axis=1, keepdims=True), axis=0, keepdims=True)


def gradient(classes, x, hots, taps_one, taps_two, small, refs, send_small, send_first, send_second):
    xs, xl, ys, yl, gs, gl, w_one, w_two, w_back, turned_x, turned_y = refs
    images = hots[0].shape[0]
    norms = norm_rows(small)
    outs = [{} for _ in x]
    put_weights(w_one, taps_one)
    parts = [
        part_gradient(classes, i, x[i], hots[i], small, norms,
                      (xs[i], xl[i], ys[i], yl[i], gs[i], gl[i], w_one, w_two, w_back, turned_y), outs[i])
        for i in range(len(x))
    ]
    step(*parts)
    step(*parts)
    taps = taps_two()
    put_weights(w_two, taps)
    step(*parts)
    put_weights(w_back, [tap.T for tap in reversed(taps)])
    step(*parts)
    send_second(kernel_grad(turned_y, gs, gl, images))
    step(*parts)
    step(*parts)
    total = {key: sum(out[key] for out in outs[1:]) + outs[0][key] for key in ("norms", "head", "bias", "cross")}
    extras = jnp.concatenate([total["bias"], jnp.broadcast_to(total["cross"], (1, 112))], axis=1)
    grads_one = kernel_grad(turned_x, ys, yl, images, range(2))
    send_first(0, grads_one)
    send_first(1, grads_one + kernel_grad(turned_x, ys, yl, images, range(2, 3)))
    send_small(jnp.concatenate([small_block(total["norms"], total["head"]), extras], axis=0))


def greet(axes):
    barrier = pltpu.get_barrier_semaphore()
    count = 0
    for axis in axes:
        n = lax.axis_size(axis)
        me = lax.axis_index(axis)
        for k in range(1, n):
            pl.semaphore_signal(barrier, inc=1, device_id={axis: lax.rem(me + k, n)}, device_id_type=MESH)
        count += n - 1
    return lambda: pl.semaphore_wait(barrier, count)


def partner(me, k, n):
    if n & (n - 1):
        return lax.rem(me + k, n)
    peer, bit = me, 1
    while bit <= k:
        if k & bit:
            peer = peer + bit - 2 * bit * lax.rem(lax.div(me, bit), 2)
        bit *= 2
    return peer


def send_all(axis, source, slot, send_sem, recv_sem):
    n = lax.axis_size(axis)
    me = lax.axis_index(axis)
    copies = []
    for k in reversed(range(1, n)):
        peer = partner(me, k, n)
        copy = pltpu.make_async_remote_copy(
            src_ref=source(peer), dst_ref=slot(me), send_sem=send_sem.at[k], recv_sem=recv_sem.at[k],
            device_id={axis: peer}, device_id_type=MESH,
        )
        copy.start()
        copies.append(copy)
    return copies


def leave(copies):
    for copy in copies:
        copy.wait_send()


def arrive(copies):
    for copy in copies:
        copy.wait_recv()


def finish(copies):
    arrive(copies)
    leave(copies)


def in_order(ref):
    total = ref[0]
    for s in range(1, ref.shape[0]):
        total = total + ref[s]
    return total


def all_sum(value):
    while value.ndim > 2:
        value = jnp.sum(value, axis=0)
    return jnp.sum(jnp.sum(value, axis=0, keepdims=True), axis=1, keepdims=True)


def square_sum(value):
    return all_sum(value * value)


def whole_kernel(classes, step_size, x_hbm, label_hbm, test_hbm, first_hbm, second_hbm, norms_hbm, head_hbm, bias_hbm,
                 mom_first_hbm, mom_second_hbm, mom_norm_hbm, mom_head_hbm, mom_bias_hbm,
                 mean, hamiltonians, potentials, forces,
                 x_raw, label_ref, test_raw, first, second, norms, head, bias,
                 mom_first, mom_second, mom_norm, mom_head, mom_bias, load_sem,
                 x_ref, test_ref, xs, xl, ys, yl, gs, gl, ts, tl, us, ul, w_one, w_two, w_back, turned_x, turned_y,
                 square, small_all, small_mom, out_small, got_small, outs, gots, mines, alls, moms,
                 part, parts, probs_own, seen,
                 send_s, recv_s, send_g, recv_g, send_t, recv_t, send_d, recv_d, send_e, recv_e):
    loads = [
        pltpu.make_async_copy(source, target, load_sem.at[i])
        for i, (source, target) in enumerate(
            (
                (x_hbm, x_raw), (first_hbm, first), (norms_hbm, norms), (head_hbm, head), (bias_hbm, bias),
                (label_hbm, label_ref), (second_hbm, second), (mom_first_hbm, mom_first), (mom_second_hbm, mom_second),
                (mom_norm_hbm, mom_norm), (mom_head_hbm, mom_head), (mom_bias_hbm, mom_bias), (test_hbm, test_raw),
            )
        )
    ]
    for load in loads:
        load.start()
    n = lax.axis_size("dp")
    me = lax.axis_index("dp")
    chain = lax.axis_index("chain")
    per = CH // n
    arrived = greet(("dp", "chain"))
    h = step_size[0]
    images = label_ref.shape[1]
    some = images // PARTS
    tests = mean.shape[0]
    pairs = x_ref[0].shape[0]
    for ref in xs + xl + ys + yl + gs + gl:
        clear_edges(ref, some)
    for load in loads[0:6]:
        load.wait()
    load_maps(x_raw, x_ref, some)
    spots = jnp.broadcast_to(label_ref[...], (128, images)) == lax.broadcasted_iota(jnp.int32, (128, images), 0)
    hot = jnp.where(spots, 1.0, 0.0).T[:, 0:16]
    hots = [hot[i * some : (i + 1) * some] for i in range(PARTS)]
    for i in range(PARTS):
        put_turned(turned_x, put_windows(xs[i], xl[i], [x_ref[i][p] for p in range(pairs)], some), i)
    small_all[0] = pack_small(norms, head, bias, square)
    for load in loads[6:]:
        load.wait()
    refs = (xs, xl, ys, yl, gs, gl, w_one, w_two, w_back, turned_x, turned_y)
    kernels, kernel_moms = (first, second), (mom_first, mom_second)
    taps_one = [first[0, t] for t in range(TAPS)]
    taps_two = lambda: [second[0, t] for t in range(TAPS)]
    shares = [None] * len(GROUPS)
    force = [None] * len(GROUPS)
    kinetic = [None] * len(GROUPS)
    for stage, factor in enumerate((0.5, 1.0, 0.5)):
        small = small_all.at[stage]
        copies = {}

        def send_group(g, grads):
            put_grads(outs[g], grads, *GROUPS[g][1:])
            copies[g] = send_all("dp", lambda s: outs[g].at[s], lambda s: gots[g].at[stage, s],
                                 send_g.at[stage, g], recv_g.at[stage, g])

        def send_small(block):
            out_small[...] = block
            copies["small"] = send_all("dp", lambda s: out_small, lambda s: got_small.at[stage, s],
                                       send_s.at[stage], recv_s.at[stage])

        def send_first(g, grads):
            send_group(g, grads)

        def send_second(grads):
            if stage == 0:
                arrived()
            send_group(2, grads)

        gradient(classes, x_ref, hots, taps_one, taps_two, small, refs, send_small, send_first, send_second)
        got_small[stage, me] = out_small[...]
        for g in range(len(GROUPS)):
            gots[g][stage, me] = outs[g][me]
        if stage == 0:
            small_mom[...] = pack_small(mom_norm, mom_head, mom_bias, square)
            for g, (which, low, high) in enumerate(GROUPS):
                shares[g] = own_share(kernels[which], me, per, low, high)
                moms[g][...] = own_share(kernel_moms[which], me, per, low, high)
            theta_squares = square_sum(first[0]) + square_sum(second[0]) + square_sum(small[...])
            mom_squares = square_sum(mom_first[0]) + square_sum(mom_second[0]) + square_sum(small_mom[...])
            load_maps(test_raw, test_ref, tests // PARTS)
        if stage == 1:
            for ref in ts + tl + us + ul:
                clear_edges(ref, tests // PARTS)
            for i in range(PARTS):
                put_windows(ts[i], tl[i], [test_ref[i][p] for p in range(pairs)], tests // PARTS)
        if stage == 2:
            logits = test_logits(test_ref, small, tests // PARTS, (ts, tl, us, ul, w_one, w_two))
            probs = soft(logits, classes)[0]
            probs_own[...] = jnp.concatenate([probs, jnp.zeros((tests, 112), F32)], axis=1)
            others = send_all("chain", lambda s: probs_own, lambda s: seen.at[s], send_d, recv_d)
            seen[chain] = probs_own[...]
            share_squares = sum(jnp.sum(share * share, axis=0, keepdims=True) for share in shares)
        weight = 0.5 if stage != 1 else 1.0
        theta_copies = [None] * len(GROUPS)

        def take_group(g):
            which, low, high = GROUPS[g]
            finish(copies[g])
            sums = in_order(gots[g].at[stage])
            grad = sums + shares[g]
            following = moms[g][...] - (factor * h) * grad
            if stage < 2:
                shares[g] = shares[g] + h * following
                mines[g][...] = shares[g]
                theta_copies[g] = send_all("dp", lambda s: mines[g], lambda s: alls[g].at[stage, s],
                                           send_t.at[stage, g], recv_t.at[stage, g])
                alls[g][stage, me] = shares[g]
                moms[g][...] = following
            else:
                kinetic[g] = jnp.sum(following * following, axis=0, keepdims=True)
            force[g] = weight * grad if force[g] is None else force[g] + weight * grad

        for g in range(len(GROUPS)):
            take_group(g)
        finish(copies["small"])
        sums = in_order(got_small.at[stage])
        extras = sums[8:SUMS]
        small_sums = jnp.concatenate([sums[0:8], bias_rows(extras[:, 0:16])], axis=0)
        small_next = small_mom[...] - (factor * h) * (small_sums + small[...])
        if stage < 2:
            small_all[stage + 1] = small[...] + h * small_next
            small_mom[...] = small_next
        if stage == 0:
            energy_start = extras[:, 32:33] + 0.5 * theta_squares
        if stage < 2:
            def gathered(which, copies, stage):
                for g, group in enumerate(GROUPS):
                    if group[0] == which:
                        finish(copies[g])
                return load_taps([(low, high, alls[g].at[stage]) for g, (k, low, high) in enumerate(GROUPS) if k == which])

            taps_one = gathered(0, theta_copies, stage)
            taps_two = functools.partial(gathered, 1, theta_copies, stage)
    part[...] = jnp.concatenate([sum(kinetic), share_squares, jnp.zeros((6, 128), F32)], axis=0)
    copies = send_all("dp", lambda s: part, lambda s: parts.at[s], send_e, recv_e)
    parts[me] = part[...]
    for g, group in enumerate(GROUPS):
        put_forces(forces, force[g], per, *group)
    finish(others)
    mean[...] = in_order(seen) / lax.axis_size("chain")
    small_squares = square_sum(small_all[2])
    kinetic_small = square_sum(small_next)
    finish(copies)
    both = in_order(parts)
    energy_end = extras[:, 32:33] + 0.5 * (all_sum(both[1:2]) + small_squares)
    pot = jnp.concatenate([energy_start, energy_end], axis=1)
    potentials[...] = pot
    hamiltonians[...] = pot + 0.5 * jnp.concatenate([mom_squares, all_sum(both[0:1]) + kinetic_small], axis=1)


def deliver_kernel(mean, hamiltonians, potentials, forces, mean_out, hamiltonians_out, potentials_out, forces_out):
    mean_out[...] = mean[...].T[0 : mean_out.shape[0]]
    hamiltonians_out[...] = hamiltonians[...]
    potentials_out[...] = potentials[...]
    forces_out[...] = forces[...]


def vmem():
    return pl.BlockSpec(memory_space=pltpu.VMEM)


def shards(train_features, train_labels, test_features, *rest):
    n = lax.axis_size("dp")
    chains = lax.axis_size("chain")
    per = CH // n
    classes = rest[3].shape[2]
    images, height, width, _ = train_features.shape
    tests = test_features.shape[0]
    first, second, norms, head, bias, mom_first, mom_second, mom_norm, mom_head, mom_bias, step_size = rest

    def lead(array, order):
        return jnp.transpose(array, order)

    arrays = (train_features, jnp.reshape(train_labels, (1, images)), test_features,
              first, second, lead(norms, (1, 0, 2)), lead(head, (2, 0, 1)), bias,
              mom_first, mom_second, lead(mom_norm, (1, 0, 2)), lead(mom_head, (2, 0, 1)), mom_bias)
    pairs = width // 2

    def shape(*dims):
        return jax.ShapeDtypeStruct(dims, F32)

    def buffer(*dims):
        return pltpu.VMEM(dims, F32)

    def maps(count):
        return [pltpu.VMEM((pairs, (height + 2) * count // PARTS, 256), BF16)] * PARTS

    def pair(*dims):
        return [pltpu.SemaphoreType.DMA(dims)] * 2

    def groups(*lead_dims):
        return [buffer(*lead_dims, block_rows(low, high, per), 128) for _, low, high in GROUPS]

    results = pl.pallas_call(
        functools.partial(whole_kernel, classes),
        out_shape=(shape(tests, 128), shape(1, 2), shape(1, 2), shape(1, 2, TAPS, per, 64)),
        in_specs=[pl.BlockSpec(memory_space=pltpu.SMEM)] + [pl.BlockSpec(memory_space=pl.ANY)] * len(arrays),
        out_specs=[vmem()] * 4,
        scratch_shapes=[pltpu.VMEM(array.shape, array.dtype) for array in arrays]
        + [pltpu.SemaphoreType.DMA((len(arrays),))]
        + [[buffer(pairs, height * count // PARTS, 128)] * PARTS for count in (images, tests)]
        + [maps(images)] * 6 + [maps(tests)] * 4 + [pltpu.VMEM((768, 256), BF16)] * 3
        + [pltpu.VMEM((256, pairs * height * images), BF16)] * 2
        + [buffer(8, 128), buffer(3, 16, 128), buffer(16, 128), buffer(SUMS, 128), buffer(3, n, SUMS, 128),
           groups(n), groups(3, n), groups(), groups(2, n), groups(),
           buffer(8, 128), buffer(n, 8, 128), buffer(tests, 128), buffer(chains, tests, 128)]
        + pair(3, n) + pair(3, len(GROUPS), n) + pair(2, len(GROUPS), n) + pair(chains) + pair(n),
        compiler_params=pltpu.CompilerParams(
            collective_id=0, has_side_effects=True, vmem_limit_bytes=56 << 20
        ),
        name="leapfrog",
    )(step_size, *arrays)
    mean, hamiltonians, potentials, forces = pl.pallas_call(
        deliver_kernel,
        out_shape=(shape(classes, tests), shape(1, 2), shape(1, 2), shape(1, 2, TAPS, per, 64)),
        in_specs=[vmem()] * 4,
        out_specs=[vmem()] * 4,
        name="deliver",
    )(*results)
    return mean.T, hamiltonians, potentials, forces


def solution(mesh):
    placed = (
        P("dp", None, None, None),
        P("dp"),
        P("dp", None, None, None),
        P("chain", None, None, None),
        P("chain", None, None, None),
        P("chain", None, None),
        P("chain", None, None),
        P("chain", None),
        P("chain", None, None, None),
        P("chain", None, None, None),
        P("chain", None, None),
        P("chain", None, None),
        P("chain", None),
        P("chain"),
    )
    return jax.shard_map(
        shards,
        mesh=mesh,
        in_specs=placed,
        out_specs=(
            P("dp", None),
            P("chain", None),
            P("chain", None),
            P("chain", None, None, "dp", None),
        ),
        check_vma=False,
    )
```
